768 devices in a mesh: xy: 64 (over z_hi, y, core), gz: 12 (over x, z_lo).
Axes of the slice: x: 4, y: 8, z: 12 (z_hi: 4, z_lo: 3; z = z_hi * 3 + z_lo), core: 2. Of those that a mesh axis runs over, the one named last changes fastest.
Arguments:
- positions: float32 [3, 64, 24, 32, 128], P(None, 'xy', 'gz'), may hold values from 0 to 1
- atom_types: int32 [64, 24, 32, 128], P('xy', 'gz'), may hold values from 0 to 17
- atom_counts: int32 [64, 24, 32], P('xy', 'gz'), may hold values from 32 to 128
- pair_flags: int32 [13, 64, 24, 32], P(None, 'xy', 'gz'), may hold values 0 or 1
- sigma_table: float32 [18], replicated, may hold values from 0.12 to 0.2
- epsilon_table: float32 [18], replicated, may hold values from 0.05 to 0.4
- charge_table: float32 [18], replicated, may hold values from -0.6 to 0.6
Outputs:
- forces: float32 [3, 64, 24, 32, 128], P(None, 'xy', 'gz')
The draws below stay inside these ranges and needn't reach their ends.
Inputs may be any that keep to these rules, and one draw needn't show every extreme that they name: `atom_counts`: live atoms of a block; slots from the count on are padding. `pair_flags`: 1 where the pair of a cell with its k-th half-shell neighbour is on the list.
All inputs are finite; a program needn't handle non-finite values. No bound on the sum of `pair_flags` on one device may be relied on, other than what follows from the above.
Results may differ from the reference program's by a relative error of at most 0.0001.
Values sent between devices are 32-bit elements; how exact they have to be, the bound alone decides.
A program may use at most 32 MiB of HBM per device.

```python
import math
import jax
import jax.numpy as jnp
from jax import lax

NTYPES = 18
BLOCK = 128
NYC = 32
NXC = 64
NZC = 24


def set_ends(values, key, low, top_value):
    spot = [jax.random.randint(jax.random.fold_in(key, axis), (), 0, length) for axis, length in enumerate(values.shape)]
    longest = values.shape.index(max(values.shape))
    beside = spot[:longest] + [(spot[longest] + 1) % values.shape[longest]] + spot[longest + 1:]
    return values.at[tuple(spot)].set(low).at[tuple(beside)].set(top_value)


def shard_levels(key, dims, split, least, largest):
    def one(position, parts):
        heights = jax.random.uniform(jax.random.fold_in(jax.random.fold_in(key, 6), position), (parts,), jnp.float32, least / len(split), largest / len(split))
        return jnp.repeat(jnp.exp(heights), dims[position] // parts).reshape((-1,) + (1,) * (len(dims) - position - 1))

    gain = one(*split[0])
    for cut in split[1:]:
        gain = gain * one(*cut)
    return gain


def setup_inputs(seed: int = 0) -> dict:
    seeds = jax.random.split(jax.random.key(seed), 8)
    return {
        "positions": jnp.clip(1.0 * jax.random.uniform(seeds[0], (3, NXC, NZC, NYC, BLOCK), jnp.float32) ** shard_levels(seeds[0], (3, NXC, NZC, NYC, BLOCK), ((1, 64), (2, 12)), -0.2, 0.2), 0.0, 1.0),
        "atom_types": set_ends(jax.random.randint(seeds[1], (NXC, NZC, NYC, BLOCK), 0, NTYPES), jax.random.fold_in(seeds[1], 1), 0, NTYPES - 1).astype(jnp.int32),
        "atom_counts": set_ends(jax.random.randint(seeds[2], (NXC, NZC, NYC), BLOCK // 4, BLOCK + 1), jax.random.fold_in(seeds[2], 1), BLOCK // 4, BLOCK).astype(jnp.int32),
        "pair_flags": set_ends((jax.random.randint(seeds[3], (13, NXC, NZC, NYC), 0, 4) < 3).astype(jnp.int32), jax.random.fold_in(seeds[3], 1), 0, 1),
        "sigma_table": jnp.clip(jax.random.uniform(seeds[4], (NTYPES,), jnp.float32, 0.12, 0.2), 0.12, 0.2),
        "epsilon_table": jnp.clip(jnp.exp(jax.random.uniform(seeds[5], (NTYPES,), jnp.float32, math.log(0.05), math.log(0.4))), 0.05, 0.4),
        "charge_table": jnp.clip(jax.random.uniform(seeds[6], (NTYPES,), jnp.float32, -0.6, 0.6), -0.6, 0.6),
    }


SOFTENING = 0.0125
SCREENING = 4.0
CUT_SCALE = 4.0
HALF_SHELL = ((0, 0, 1), (0, 1, -1), (0, 1, 0), (0, 1, 1), (1, -1, -1), (1, -1, 0), (1, -1, 1), (1, 0, -1), (1, 0, 0), (1, 0, 1), (1, 1, -1), (1, 1, 0), (1, 1, 1))

def atom_table(positions, atom_types, atom_counts, sigma_table, epsilon_table, charge_table):
    block_size = positions.shape[-1]
    type_ids = jnp.arange(sigma_table.shape[0], dtype=jnp.int32)
    onehot = (atom_types[None] == type_ids[:, None, None, None, None]).astype(jnp.float32)
    slot_ids = jnp.arange(block_size, dtype=jnp.int32)
    present = (slot_ids[None, None, None, :] < atom_counts[:, :, :, None]).astype(jnp.float32)
    sigma_atom = lax.optimization_barrier(jnp.sum(onehot * sigma_table[:, None, None, None, None], axis=0))
    well_root = lax.optimization_barrier(jnp.sum(onehot * jnp.sqrt(epsilon_table)[:, None, None, None, None], axis=0)) * present
    charge = lax.optimization_barrier(jnp.sum(onehot * charge_table[:, None, None, None, None], axis=0)) * present
    return jnp.concatenate([positions, sigma_atom[None], well_root[None], charge[None]], axis=0)

def pair_tiles(near_block, far_block, offset, weight_mask):
    delta_x = near_block[0][:, :, None] - far_block[0][:, None, :] - offset[0]
    delta_y = near_block[1][:, :, None] - far_block[1][:, None, :] - offset[1]
    delta_z = near_block[2][:, :, None] - far_block[2][:, None, :] - offset[2]
    dist_sq = delta_x * delta_x + delta_y * delta_y + delta_z * delta_z
    sigma_pair = 0.5 * (near_block[3][:, :, None] + far_block[3][:, None, :])
    sigma_sq = sigma_pair * sigma_pair
    well_depth = near_block[4][:, :, None] * far_block[4][:, None, :]
    charges = near_block[5][:, :, None] * far_block[5][:, None, :]
    shifted = dist_sq + sigma_sq
    quotient = sigma_sq / shifted
    power_six = quotient * quotient * quotient
    dispersion = 4.0 * well_depth * (power_six * power_six - power_six)
    dispersion_slope = -12.0 * well_depth * power_six * (2.0 * power_six - 1.0) / shifted
    radius = jnp.sqrt(dist_sq + SOFTENING)
    damping = jnp.exp(-SCREENING * radius)
    coulomb = charges * damping / radius
    coulomb_slope = -charges * damping * (SCREENING * radius + 1.0) / (2.0 * radius * radius * radius)
    switch = jnp.maximum(1.0 - CUT_SCALE * dist_sq, 0.0)
    scalar = -2.0 * ((dispersion_slope + coulomb_slope) * switch * switch - 2.0 * CUT_SCALE * switch * (dispersion + coulomb))
    scalar = scalar * weight_mask
    deltas = (delta_x, delta_y, delta_z)
    on_near = jnp.stack([lax.optimization_barrier(jnp.sum(scalar * component, axis=2)) for component in deltas])
    on_far = -jnp.stack([lax.optimization_barrier(jnp.sum(scalar * component, axis=1)) for component in deltas])
    return (on_near, on_far)

def sweep(own_block, neighbours, flag_rows, offsets, masks, group_limit):
    cell_total = own_block.shape[1]
    block_size = own_block.shape[2]
    group_size = math.gcd(cell_total, group_limit)
    direction_total = len(offsets)

    def visit(step_index, carried):
        first_cell = (step_index * group_size).astype(jnp.int32)
        near_block = lax.dynamic_slice_in_dim(own_block, first_cell, group_size, 1)
        on_block = jnp.zeros((3, group_size, block_size), jnp.float32)
        returned = []
        for direction in range(direction_total):
            remote = lax.dynamic_slice_in_dim(neighbours[direction], first_cell, group_size, 1)
            listed = lax.dynamic_slice_in_dim(flag_rows[direction], first_cell, group_size, 0)
            weight_mask = listed[:, None, None]
            if masks[direction] is not None:
                weight_mask = weight_mask * masks[direction][None]
            on_near, on_far = pair_tiles(near_block, remote, offsets[direction], weight_mask)
            on_block = on_block + on_near
            returned.append(on_far)
        forces = lax.dynamic_update_slice_in_dim(carried[0], on_block, first_cell, 1)
        backs = lax.dynamic_update_slice_in_dim(carried[1], jnp.stack(returned), first_cell, 2)
        return (forces, backs)
    initial = (jnp.zeros((3, cell_total, block_size), jnp.float32), jnp.zeros((direction_total, 3, cell_total, block_size), jnp.float32))
    return lax.fori_loop(0, cell_total // group_size, visit, initial)

def reference(positions, atom_types, atom_counts, pair_flags, sigma_table, epsilon_table, charge_table):
    atom_data = atom_table(positions, atom_types, atom_counts, sigma_table, epsilon_table, charge_table)
    columns = positions.shape[1]
    layers = positions.shape[2]
    rows_y = positions.shape[3]
    block_size = positions.shape[4]
    cell_total = columns * layers * rows_y
    flattened = atom_data.reshape(6, cell_total, block_size)
    slot_ids = jnp.arange(block_size, dtype=jnp.int32)
    upper = (slot_ids[None, :] > slot_ids[:, None]).astype(jnp.float32)
    listed = jnp.concatenate([jnp.ones((1, cell_total), jnp.float32), pair_flags.reshape(13, cell_total).astype(jnp.float32)], axis=0)
    offsets = ((0, 0, 0),) + HALF_SHELL
    result = jnp.zeros((3, columns, layers, rows_y, block_size), jnp.float32)
    for direction in range(14):
        shift_x, shift_y, shift_z = offsets[direction]
        remote = jnp.roll(atom_data, (-shift_x, -shift_z, -shift_y), axis=(1, 2, 3)).reshape(1, 6, cell_total, block_size)
        chosen = upper if direction == 0 else None
        forces, backs = sweep(flattened, remote, listed[direction:direction + 1], (offsets[direction],), [chosen], 256)
        moved = jnp.roll(backs[0].reshape(3, columns, layers, rows_y, block_size), (shift_x, shift_z, shift_y), axis=(1, 2, 3))
        result = result + forces.reshape(3, columns, layers, rows_y, block_size) + moved
    return result
```

```python
import functools

import jax
import jax.numpy as jnp
from jax import lax
from jax.experimental import pallas as pl
from jax.experimental.pallas import tpu as pltpu
from jax.sharding import PartitionSpec as P

SOFTENING = 0.0125
HALF_SHELL = (
    (0, 0, 1),
    (0, 1, -1),
    (0, 1, 0),
    (0, 1, 1),
    (1, -1, -1),
    (1, -1, 0),
    (1, -1, 1),
    (1, 0, -1),
    (1, 0, 0),
    (1, 0, 1),
    (1, 1, -1),
    (1, 1, 0),
    (1, 1, 1),
)
OCTANTS = (
    (0, 0, 0),
    (0, 0, 1),
    (0, 1, 1),
    (0, 1, 0),
    (1, 1, 0),
    (1, 1, 1),
    (1, 0, 1),
    (1, 0, 0),
)
FLAG_LANE = 16
COUNT_LANE = FLAG_LANE + 13
ROW_BLOCKS = (4, 6, 8, 10, 12, 14, 16)


def octant_runs(offset):
    wanted = [
        all(o == 0 or (o < 0) == bool(bit) for o, bit in zip(offset, octant)) for octant in OCTANTS
    ]
    runs, start = [], None
    for place, keep in enumerate(wanted + [False]):
        if keep and start is None:
            start = place
        if not keep and start is not None:
            runs.append((start, place))
            start = None
    return runs


SEGMENTS = [((0, 0, 0), (0, 8), None, False)]
for _k, _offset in enumerate(HALF_SHELL):
    for _sign in (1, -1):
        _reach = tuple(_sign * o for o in _offset)
        for _run in octant_runs(_reach):
            SEGMENTS.append((_reach, _run, _k, _sign < 0))


def looked_up(types, tables):
    values = [jnp.zeros(types.shape, jnp.float32) for _ in tables]
    for t in range(tables[0].shape[0]):
        here = types == t
        values = [jnp.where(here, table[t], value) for table, value in zip(tables, values)]
    sigma, epsilon, charge = values
    return [0.5 * sigma, jnp.sqrt(8.0 * epsilon), charge]


ROWS = 32
LAYER_ROWS = 4 * ROWS + 8
ROUTE = (
    (0, (0, -1), 5, 7),
    (0, (-1, 0), 5, 9),
    (0, (1, 0), 5, 1),
    (1, (0, 1), 6, 4),
    (1, (-1, 0), 6, 10),
    (1, (1, 0), 6, 2),
    (2, (-1, 0), 7, 11),
    (2, (1, 0), 7, 3),
    (3, (-1, 0), 4, 8),
    (3, (1, 0), 4, 0),
)


def sort_kernel(
    sigma_ref,
    epsilon_ref,
    charge_ref,
    pos_ref,
    type_ref,
    count_ref,
    flag_ref,
    ghost_ref,
    near_ref,
    piece_ref,
    rank_ref,
    meta_ref,
    send_sem,
    recv_sem,
    *,
    sizes,
):
    cells, block = type_ref.shape
    rows = ROWS
    copies = []
    if sizes is not None:
        mine = [lax.axis_index("xy"), lax.axis_index("gz")]

        def at(steps):
            return tuple(lax.rem(m + d + n, n) for m, d, n in zip(mine, steps, sizes))

        barrier = pltpu.get_barrier_semaphore()
        for steps in ((0, -1), (0, 1), (-1, 0), (1, 0)):
            pl.semaphore_signal(
                barrier, inc=1, device_id=at(steps), device_id_type=pl.DeviceIdType.MESH
            )
        for index, (_, steps, source, target) in enumerate(ROUTE):
            copies.append(
                pltpu.make_async_remote_copy(
                    src_ref=ghost_ref.at[source],
                    dst_ref=ghost_ref.at[target],
                    send_sem=send_sem.at[index],
                    recv_sem=recv_sem.at[index],
                    device_id=at(steps),
                    device_id_type=pl.DeviceIdType.MESH,
                )
            )

    def send(stage):
        for copy, message in zip(copies, ROUTE):
            if message[0] == stage:
                copy.start()

    lane = lax.broadcasted_iota(jnp.int32, (cells, block), 1)
    spread_row = lax.broadcasted_iota(jnp.int32, (16, block), 0)
    spread_lane = lax.broadcasted_iota(jnp.int32, (16, block), 1)
    spread = jnp.where(spread_row + FLAG_LANE == spread_lane, 1.0, 0.0).astype(jnp.bfloat16)
    aux = []
    for layer in range(2):
        small = jnp.concatenate(
            [
                flag_ref[:, layer, :].astype(jnp.float32),
                count_ref[layer : layer + 1, :].astype(jnp.float32),
                jnp.zeros((2, rows), jnp.float32),
            ],
            axis=0,
        )
        aux.append(
            lax.dot_general(
                small.astype(jnp.bfloat16),
                spread,
                (((0,), (0,)), ((), ())),
                preferred_element_type=jnp.float32,
            )
        )
    aux = jnp.concatenate(aux, axis=0)
    count = jnp.broadcast_to(aux[:, COUNT_LANE : COUNT_LANE + 1], (cells, block))
    live = lane.astype(jnp.float32) < count
    types = type_ref[...]
    positions = [pos_ref[c] for c in range(3)]
    upper = [jnp.where(p >= 0.5, 1, 0) for p in positions]
    mid = upper[0] ^ upper[1]
    code = 4 * upper[0] + 2 * mid + (mid ^ upper[2])
    code = jnp.where(live, code, 8)
    row_id = lax.broadcasted_iota(jnp.int32, (block, 2 * block), 0)
    lane_id = lax.broadcasted_iota(jnp.int32, (block, 2 * block), 1)
    counting = jnp.where((row_id <= lane_id) | (lane_id >= block), 1.0, 0.0).astype(jnp.bfloat16)
    rank = jnp.zeros((cells, block), jnp.float32)
    offset = jnp.zeros((cells, block), jnp.float32)
    meta = aux
    for b in range(9):
        member = code == b
        found = jnp.dot(
            jnp.where(member, 1.0, 0.0).astype(jnp.bfloat16),
            counting,
            preferred_element_type=jnp.float32,
        )
        rank = jnp.where(member, found[:, :block] - 1.0 + offset, rank)
        meta = jnp.where(lane == b, offset, meta)
        offset = offset + found[:, block:]
    rank_ref[...] = rank
    meta_ref[...] = jnp.where(lane < 32, meta, 0.0)
    for layer in range(2):
        packed = meta_ref[pl.ds(layer * rows, 8, stride=4), :]
        for part in range(1, 4):
            packed = packed + pltpu.roll(
                meta_ref[pl.ds(layer * rows + part, 8, stride=4), :], 32 * part, axis=1
            )
        ghost_ref[5 + layer, 4 * rows : LAYER_ROWS, :] = packed
    zero = jnp.zeros((cells, block), jnp.float32)
    high = [p.astype(jnp.bfloat16).astype(jnp.float32) for p in positions]
    rest = [p - h for p, h in zip(positions, high)]
    middle = [r.astype(jnp.bfloat16).astype(jnp.float32) for r in rest]
    low = [r - m for r, m in zip(rest, middle)]
    pieces = (
        high + [types.astype(jnp.float32)] + middle + [zero] + low + [zero, zero, zero, zero, zero]
    )
    for group in range(cells // 8):
        part = slice(group * 8, group * 8 + 8)
        for c in range(16):
            piece_ref[pl.ds(group * 128 + c, 8, stride=16), :] = pieces[c][part]
    slot = lax.broadcasted_iota(jnp.int32, (block, block), 0).astype(jnp.float32)

    def sort_layer(layer):
        def one(row, carry):
            cell = layer * rows + row
            ranks = jnp.broadcast_to(rank_ref[pl.ds(cell, 1), :], (block, block))
            chosen = jnp.where(ranks == slot, 1.0, 0.0).astype(jnp.bfloat16)
            data = piece_ref[pl.ds(pl.multiple_of(cell * 16, 16), 16), :].astype(jnp.bfloat16)
            moved = lax.dot_general(
                data, chosen, (((1,), (1,)), ((), ())), preferred_element_type=jnp.float32
            )
            whole = (moved[0:4] + moved[4:8]) + moved[8:12]
            for c in range(4):
                ghost_ref[5 + layer, pl.ds(c * rows + row, 1), :] = whole[c : c + 1]
            return carry

        lax.fori_loop(0, rows, one, 0, unroll=4)

    sort_layer(0)
    if copies:
        pl.semaphore_wait(barrier, 4)
    send(0)
    sort_layer(1)
    send(1)
    present = jnp.where(live, 1.0, 0.0)
    kinds = looked_up(types, (sigma_ref, epsilon_ref, charge_ref))
    near = positions + [kinds[0], kinds[1] * present, kinds[2] * present, zero, zero]
    for group in range(cells // 8):
        part = slice(group * 8, group * 8 + 8)
        for c in range(8):
            near_ref[pl.ds(group * 64 + c, 8, stride=8), :] = near[c][part]
    if copies:
        copies[0].wait()
        send(2)
        copies[3].wait()
        send(3)
        for index in (1, 2, 4, 5, 6, 7, 8, 9):
            copies[index].wait()


def pair_force(near, far):
    delta = [near[c] - far[c] for c in range(3)]
    dist_sq = delta[0] * delta[0] + delta[1] * delta[1] + delta[2] * delta[2]
    sigma = near[3] + far[3]
    sigma_sq = sigma * sigma
    inverse = 1.0 / (dist_sq + sigma_sq)
    quotient = sigma_sq * inverse
    power = quotient * quotient * quotient
    softened = dist_sq + SOFTENING
    inverse_radius = lax.rsqrt(softened)
    reach = (softened * inverse_radius) * -4.0
    switch = jnp.maximum(1.0 - 4.0 * dist_sq, 0.0)
    well = (near[4] * far[4]) * power
    screened = (near[5] * far[5]) * (jnp.exp(reach) * inverse_radius)
    lennard = well * ((8.0 * power - 8.0) + (switch * inverse) * (6.0 * power - 3.0))
    coulomb = screened * (
        16.0 + (switch * (1.0 - reach)) * (inverse_radius * inverse_radius)
    )
    scalar = (lennard + coulomb) * switch
    return [scalar * d for d in delta]


def pair_kernel(
    sigma_ref,
    epsilon_ref,
    charge_ref,
    ghost_ref,
    near_ref,
    out_ref,
    far_ref,
    shift_ref,
    list_ref,
    wide_ref,
    pick_ref,
    sum_ref,
    turned_ref,
    whole_ref,
    meta_ref,
    meta_sem,
):
    layers, rows = 2, ROWS
    block = 128
    places = ghost_ref.shape[0]
    for place in range(places):
        whole_ref[8 * place : 8 * place + 8, :] = ghost_ref[place, 4 * rows : LAYER_ROWS, :].astype(
            jnp.int32
        )
    starts = pltpu.make_async_copy(whole_ref, meta_ref, meta_sem)
    starts.start()

    def listed(cell, what):
        return meta_ref[cell >> 2, ((cell & 3) << 5) + what]

    tile = (8, block)
    lane = lax.broadcasted_iota(jnp.int32, tile, 1)
    sub = lax.broadcasted_iota(jnp.int32, tile, 0)

    def fill(group, carry):
        place, first = group // 4, pl.multiple_of((group % 4) * 8, 8)
        parts = [ghost_ref[place, pl.ds(c * rows + first, 8), :] for c in range(4)]
        values = parts[:3] + looked_up(parts[3], (sigma_ref, epsilon_ref, charge_ref))
        for c, value in enumerate(values):
            far_ref[pl.ds(group * 64 + c, 8, stride=8), :] = value
        return carry

    lax.fori_loop(0, places * rows // 8, fill, 0, unroll=2)
    for index in range(27):
        step = (index // 9 - 1, (index // 3) % 3 - 1, index % 3 - 1)
        shift_ref[index * 8 : index * 8 + 8, :] = jnp.where(
            sub == 0,
            float(step[0]),
            jnp.where(sub == 1, float(step[1]), jnp.where(sub == 2, float(step[2]), 0.0)),
        )
    turned_ref[...] = jnp.zeros(turned_ref.shape, jnp.float32)
    piece = lax.broadcasted_iota(jnp.int32, (32, 6 * block), 0)
    column = lax.broadcasted_iota(jnp.int32, (32, 6 * block), 1)
    pick_ref[...] = jnp.where(
        ((piece & 7) == (column >> 7)) & (piece < 24), 1.0, 0.0
    ).astype(jnp.bfloat16)

    starts.wait()

    def visit(cell, carry):
        layer = cell // rows
        row = cell % rows
        home = (4 + layer + 1) * rows + row
        live = listed(home, 8)
        current = jnp.zeros(tile, jnp.float32)
        filled = jnp.int32(0)
        for (dx, dy, dz), (first, last), k, backward in SEGMENTS:
            other = ((dx + 1) * 4 + layer + 1 + dz) * rows + ((row + dy) & (rows - 1))
            start = listed(other, first)
            length = listed(other, last) - start
            if k is not None:
                length = length * listed(other if backward else home, FLAG_LANE + k)
            value = far_ref[pl.ds(pl.multiple_of(other * 8, 8), 8), :]
            if k is not None:
                index = (dx + 1) * 9 + (dy + 1) * 3 + dz + 1
                value = value + shift_ref[index * 8 : index * 8 + 8, :]
            inside = filled & (block - 1)
            rolled = pltpu.roll(value, (inside - start) & (block - 1), axis=1)
            current = jnp.where(lane >= inside, rolled, current)
            place = filled >> 7
            list_ref[pl.ds(pl.multiple_of(place * 8, 8), 8), :] = current
            filled = filled + length
            current = jnp.where((filled >> 7) > place, rolled, current)
        current = jnp.where(lane < (filled & (block - 1)), current, 0.0)
        list_ref[pl.ds(pl.multiple_of((filled >> 7) * 8, 8), 8), :] = current
        pieces = (filled + block - 1) >> 7
        whole = near_ref[pl.ds(pl.multiple_of(cell * 8, 8), 8), :]
        high = whole.astype(jnp.bfloat16).astype(jnp.float32)
        rest = whole - high
        middle = rest.astype(jnp.bfloat16).astype(jnp.float32)
        parts = jnp.concatenate([high, middle, rest - middle, jnp.zeros(tile, jnp.float32)], axis=0)
        upright = jnp.transpose(parts).astype(jnp.bfloat16)
        wide_ref[...] = jnp.dot(upright, pick_ref[...], preferred_element_type=jnp.float32)

        for which, blocks in enumerate(ROW_BLOCKS):
            least = 8 * ROW_BLOCKS[which - 1] if which else -1

            @pl.when((live > least) & (live <= 8 * blocks))
            def _():
                for b in range(blocks):
                    for c in range(3):
                        sum_ref[c, 8 * b : 8 * b + 8, :] = jnp.zeros(tile, jnp.float32)

                def against(piece, inner):
                    far = [
                        jnp.broadcast_to(list_ref[pl.ds(piece * 8 + c, 1), :], tile)
                        for c in range(6)
                    ]
                    for b in range(blocks):
                        part = slice(8 * b, 8 * b + 8)
                        near = [wide_ref[part, c * block : (c + 1) * block] for c in range(6)]
                        for c, value in enumerate(pair_force(near, far)):
                            sum_ref[c, part, :] += value
                    return inner

                lax.fori_loop(0, pieces, against, 0)
                for b in range(blocks):
                    part = slice(8 * b, 8 * b + 8)
                    for c in range(3):
                        force = jnp.sum(sum_ref[c, part, :], axis=1, keepdims=True)
                        turned_ref[c, part, :] = jnp.where(
                            lane == cell, force, turned_ref[c, part, :]
                        )

        return carry

    lax.fori_loop(0, layers * rows, visit, 0)
    for c in range(3):
        out_ref[c] = jnp.transpose(turned_ref[c])[: layers * rows]


def sort_cells(tables, positions, types, counts, flags, sizes=None):
    cells, block = types.shape
    smem = pl.BlockSpec(memory_space=pltpu.SMEM)
    vmem = pl.BlockSpec(memory_space=pltpu.VMEM)
    return pl.pallas_call(
        functools.partial(sort_kernel, sizes=sizes),
        out_shape=(
            jax.ShapeDtypeStruct((12, LAYER_ROWS, block), jnp.float32),
            jax.ShapeDtypeStruct((8 * cells, block), jnp.float32),
        ),
        in_specs=[smem, smem, smem, vmem, vmem, vmem, vmem],
        out_specs=(vmem, vmem),
        scratch_shapes=[
            pltpu.VMEM((16 * cells, block), jnp.float32),
            pltpu.VMEM((cells, block), jnp.float32),
            pltpu.VMEM((cells, block), jnp.float32),
            pltpu.SemaphoreType.DMA((len(ROUTE),)),
            pltpu.SemaphoreType.DMA((len(ROUTE),)),
        ],
        compiler_params=pltpu.CompilerParams(collective_id=0, has_side_effects=True)
        if sizes
        else None,
        name="sort_and_share",
    )(*tables, positions, types, counts, flags)


def pair_forces(tables, ghost, near):
    total_cells, block = ghost.shape[0] * ROWS, ghost.shape[2]
    cells = near.shape[0] // 8
    smem = pl.BlockSpec(memory_space=pltpu.SMEM)
    vmem = pl.BlockSpec(memory_space=pltpu.VMEM)
    return pl.pallas_call(
        pair_kernel,
        out_shape=jax.ShapeDtypeStruct((3, cells, block), jnp.float32),
        in_specs=[smem, smem, smem, vmem, vmem],
        out_specs=vmem,
        scratch_shapes=[
            pltpu.VMEM((8 * total_cells, block), jnp.float32),
            pltpu.VMEM((27 * 8, block), jnp.float32),
            pltpu.VMEM((28 * 8, block), jnp.float32),
            pltpu.VMEM((block, 6 * block), jnp.float32),
            pltpu.VMEM((32, 6 * block), jnp.bfloat16),
            pltpu.VMEM((3, block, block), jnp.float32),
            pltpu.VMEM((3, block, block), jnp.float32),
            pltpu.VMEM((8 * ghost.shape[0], block), jnp.int32),
            pltpu.SMEM((8 * ghost.shape[0], block), jnp.int32),
            pltpu.SemaphoreType.DMA,
        ],
        name="pair_forces",
    )(*tables, ghost, near)


def local(positions, atom_types, atom_counts, pair_flags, sigma_table, epsilon_table, charge_table):
    layers, rows, block = positions.shape[2:]
    cells = layers * rows
    tables = (sigma_table, epsilon_table, charge_table)
    ghost, near = sort_cells(
        tables,
        positions.reshape(3, cells, block),
        atom_types.reshape(cells, block),
        atom_counts.reshape(layers, rows),
        pair_flags.reshape(13, layers, rows),
        (lax.axis_size("xy"), lax.axis_size("gz")),
    )
    forces = pair_forces(tables, ghost, near)
    return forces.reshape(3, 1, layers, rows, block)


def solution(mesh):
    return jax.shard_map(
        local,
        mesh=mesh,
        in_specs=(
            P(None, "xy", "gz", None, None),
            P("xy", "gz", None, None),
            P("xy", "gz", None),
            P(None, "xy", "gz", None),
            P(),
            P(),
            P(),
        ),
        out_specs=P(None, "xy", "gz", None, None),
        check_vma=False,
    )
```

```python
import functools

import jax
import jax.numpy as jnp
import numpy as np
from jax import lax
from jax.experimental import pallas as pl
from jax.experimental.pallas import tpu as pltpu
from jax.sharding import PartitionSpec as P

SOFTENING = 0.0125
HALF_SHELL = (
    (0, 0, 1),
    (0, 1, -1),
    (0, 1, 0),
    (0, 1, 1),
    (1, -1, -1),
    (1, -1, 0),
    (1, -1, 1),
    (1, 0, -1),
    (1, 0, 0),
    (1, 0, 1),
    (1, 1, -1),
    (1, 1, 0),
    (1, 1, 1),
)
OCTANTS = (
    (0, 0, 0),
    (0, 0, 1),
    (0, 1, 1),
    (0, 1, 0),
    (1, 1, 0),
    (1, 1, 1),
    (1, 0, 1),
    (1, 0, 0),
)
FLAG_LANE = 16
COUNT_LANE = FLAG_LANE + 13
ROW_BLOCKS = (6, 8, 10, 12, 14, 16)


def octant_runs(offset):
    wanted = [
        all(o == 0 or (o < 0) == bool(bit) for o, bit in zip(offset, octant)) for octant in OCTANTS
    ]
    runs, start = [], None
    for place, keep in enumerate(wanted + [False]):
        if keep and start is None:
            start = place
        if not keep and start is not None:
            runs.append((start, place))
            start = None
    return runs


SEGMENTS = [((0, 0, 0), (0, 8), None, False)]
for _k, _offset in enumerate(HALF_SHELL):
    for _sign in (1, -1):
        _reach = tuple(_sign * o for o in _offset)
        for _run in octant_runs(_reach):
            SEGMENTS.append((_reach, _run, _k, _sign < 0))


LIVE_LANE = 40


def selection():
    table = np.zeros((27, 32, 384), np.float32)
    for j, ((dx, dy, dz), (first, last), k, backward) in enumerate(SEGMENTS):
        offset = (dx + 1) * 9 + (dy + 1) * 3 + dz + 1
        table[offset, first, j] += 1.0
        table[offset, last, 128 + j] += 1.0
        table[offset, first, 128 + j] -= 1.0
        if k is not None:
            table[offset if backward else 13, FLAG_LANE + k, 256 + j] += 1.0
    table[13, 8, LIVE_LANE] += 1.0
    return jnp.asarray(table, jnp.bfloat16)


def looked_up(types, tables):
    values = [jnp.zeros(types.shape, jnp.float32) for _ in tables]
    for t in range(tables[0].shape[0]):
        here = types == t
        values = [jnp.where(here, table[t], value) for table, value in zip(tables, values)]
    sigma, epsilon, charge = values
    return [0.5 * sigma, jnp.sqrt(8.0 * epsilon), charge]


ROWS = 32
LAYER_ROWS = 4 * ROWS + 8
ROUTE = (
    (0, (0, -1), 5, 7),
    (0, (-1, 0), 5, 9),
    (0, (1, 0), 5, 1),
    (1, (0, 1), 6, 4),
    (1, (-1, 0), 6, 10),
    (1, (1, 0), 6, 2),
    (2, (-1, 0), 7, 11),
    (2, (1, 0), 7, 3),
    (3, (-1, 0), 4, 8),
    (3, (1, 0), 4, 0),
)


def sort_kernel(
    sigma_ref,
    epsilon_ref,
    charge_ref,
    pos_ref,
    type_ref,
    count_ref,
    flag_ref,
    ghost_ref,
    near_ref,
    piece_ref,
    rank_ref,
    meta_ref,
    send_sem,
    recv_sem,
    *,
    sizes,
):
    cells, block = type_ref.shape
    rows = ROWS
    copies = []
    if sizes is not None:
        mine = [lax.axis_index("xy"), lax.axis_index("gz")]

        def at(steps):
            return tuple(lax.rem(m + d + n, n) for m, d, n in zip(mine, steps, sizes))

        barrier = pltpu.get_barrier_semaphore()
        for steps in ((0, -1), (0, 1), (-1, 0), (1, 0)):
            pl.semaphore_signal(
                barrier, inc=1, device_id=at(steps), device_id_type=pl.DeviceIdType.MESH
            )
        for index, (_, steps, source, target) in enumerate(ROUTE):
            copies.append(
                pltpu.make_async_remote_copy(
                    src_ref=ghost_ref.at[source],
                    dst_ref=ghost_ref.at[target],
                    send_sem=send_sem.at[index],
                    recv_sem=recv_sem.at[index],
                    device_id=at(steps),
                    device_id_type=pl.DeviceIdType.MESH,
                )
            )

    def send(stage):
        for copy, message in zip(copies, ROUTE):
            if message[0] == stage:
                copy.start()

    lane = lax.broadcasted_iota(jnp.int32, (cells, block), 1)
    spread_row = lax.broadcasted_iota(jnp.int32, (16, block), 0)
    spread_lane = lax.broadcasted_iota(jnp.int32, (16, block), 1)
    spread = jnp.where(spread_row + FLAG_LANE == spread_lane, 1.0, 0.0).astype(jnp.bfloat16)
    aux = []
    for layer in range(2):
        small = jnp.concatenate(
            [
                flag_ref[:, layer, :].astype(jnp.float32),
                count_ref[layer : layer + 1, :].astype(jnp.float32),
                jnp.zeros((2, rows), jnp.float32),
            ],
            axis=0,
        )
        aux.append(
            lax.dot_general(
                small.astype(jnp.bfloat16),
                spread,
                (((0,), (0,)), ((), ())),
                preferred_element_type=jnp.float32,
            )
        )
    aux = jnp.concatenate(aux, axis=0)
    count = jnp.broadcast_to(aux[:, COUNT_LANE : COUNT_LANE + 1], (cells, block))
    live = lane.astype(jnp.float32) < count
    types = type_ref[...]
    positions = [pos_ref[c] for c in range(3)]
    upper = [jnp.where(p >= 0.5, 1, 0) for p in positions]
    mid = upper[0] ^ upper[1]
    code = 4 * upper[0] + 2 * mid + (mid ^ upper[2])
    code = jnp.where(live, code, 8)
    row_id = lax.broadcasted_iota(jnp.int32, (block, 2 * block), 0)
    lane_id = lax.broadcasted_iota(jnp.int32, (block, 2 * block), 1)
    counting = jnp.where((row_id <= lane_id) | (lane_id >= block), 1.0, 0.0).astype(jnp.bfloat16)
    rank = jnp.zeros((cells, block), jnp.float32)
    offset = jnp.zeros((cells, block), jnp.float32)
    meta = aux
    for b in range(9):
        member = code == b
        found = jnp.dot(
            jnp.where(member, 1.0, 0.0).astype(jnp.bfloat16),
            counting,
            preferred_element_type=jnp.float32,
        )
        rank = jnp.where(member, found[:, :block] - 1.0 + offset, rank)
        meta = jnp.where(lane == b, offset, meta)
        offset = offset + found[:, block:]
    rank_ref[...] = rank
    meta_ref[...] = jnp.where(lane < 32, meta, 0.0)
    for layer in range(2):
        packed = meta_ref[pl.ds(layer * rows, 8, stride=4), :]
        for part in range(1, 4):
            packed = packed + pltpu.roll(
                meta_ref[pl.ds(layer * rows + part, 8, stride=4), :], 32 * part, axis=1
            )
        ghost_ref[5 + layer, 4 * rows : LAYER_ROWS, :] = packed
    zero = jnp.zeros((cells, block), jnp.float32)
    high = [p.astype(jnp.bfloat16).astype(jnp.float32) for p in positions]
    rest = [p - h for p, h in zip(positions, high)]
    middle = [r.astype(jnp.bfloat16).astype(jnp.float32) for r in rest]
    low = [r - m for r, m in zip(rest, middle)]
    pieces = (
        high + [types.astype(jnp.float32)] + middle + [zero] + low + [zero, zero, zero, zero, zero]
    )
    for group in range(cells // 8):
        part = slice(group * 8, group * 8 + 8)
        for c in range(16):
            piece_ref[pl.ds(group * 128 + c, 8, stride=16), :] = pieces[c][part]
    slot = lax.broadcasted_iota(jnp.int32, (block, block), 0).astype(jnp.float32)

    def sort_layer(layer):
        def one(row, carry):
            cell = layer * rows + row
            ranks = jnp.broadcast_to(rank_ref[pl.ds(cell, 1), :], (block, block))
            chosen = jnp.where(ranks == slot, 1.0, 0.0).astype(jnp.bfloat16)
            data = piece_ref[pl.ds(pl.multiple_of(cell * 16, 16), 16), :].astype(jnp.bfloat16)
            moved = lax.dot_general(
                data, chosen, (((1,), (1,)), ((), ())), preferred_element_type=jnp.float32
            )
            whole = (moved[0:4] + moved[4:8]) + moved[8:12]
            for c in range(4):
                ghost_ref[5 + layer, pl.ds(c * rows + row, 1), :] = whole[c : c + 1]
            return carry

        lax.fori_loop(0, rows, one, 0, unroll=4)

    sort_layer(0)
    if copies:
        pl.semaphore_wait(barrier, 4)
    send(0)
    sort_layer(1)
    send(1)
    present = jnp.where(live, 1.0, 0.0)
    kinds = looked_up(types, (sigma_ref, epsilon_ref, charge_ref))
    near = positions + [kinds[0], kinds[1] * present, kinds[2] * present, zero, zero]
    for group in range(cells // 8):
        part = slice(group * 8, group * 8 + 8)
        for c in range(8):
            near_ref[pl.ds(group * 64 + c, 8, stride=8), :] = near[c][part]
    if copies:
        copies[0].wait()
        send(2)
        copies[3].wait()
        send(3)
        for index in (1, 2, 4, 5, 6, 7, 8, 9):
            copies[index].wait()


def pair_force(near, far):
    delta = [near[c] - far[c] for c in range(3)]
    dist_sq = delta[0] * delta[0] + delta[1] * delta[1] + delta[2] * delta[2]
    sigma = near[3] + far[3]
    sigma_sq = sigma * sigma
    inverse = 1.0 / (dist_sq + sigma_sq)
    quotient = sigma_sq * inverse
    power = quotient * quotient * quotient
    softened = dist_sq + SOFTENING
    inverse_radius = lax.rsqrt(softened)
    reach = (softened * inverse_radius) * -4.0
    switch = jnp.maximum(1.0 - 4.0 * dist_sq, 0.0)
    well = (near[4] * far[4]) * power
    screened = (near[5] * far[5]) * (jnp.exp(reach) * inverse_radius)
    lennard = well * ((8.0 * power - 8.0) + (switch * inverse) * (6.0 * power - 3.0))
    coulomb = screened * (
        16.0 + (switch * (1.0 - reach)) * (inverse_radius * inverse_radius)
    )
    scalar = (lennard + coulomb) * switch
    return [scalar * d for d in delta]


def pair_kernel(
    sigma_ref,
    epsilon_ref,
    charge_ref,
    select_ref,
    ghost_ref,
    near_ref,
    out_ref,
    far_ref,
    shift_ref,
    list_ref,
    wide_ref,
    pick_ref,
    up_ref,
    sum_ref,
    turned_ref,
    open_ref,
    plan_ref,
    steps_ref,
    steps_sem,
):
    layers, rows = 2, ROWS
    block = 128
    places = ghost_ref.shape[0]
    for place in range(places):
        packed = ghost_ref[place, 4 * rows : LAYER_ROWS, :]
        for part in range(4):
            turned = pltpu.roll(packed, (block - 32 * part) % block, axis=1) if part else packed
            open_ref[place, pl.ds(8 + part, 8, stride=4), :] = turned
        open_ref[place, 7:8, :] = open_ref[place, 39:40, :]
        open_ref[place, 40:41, :] = open_ref[place, 8:9, :]
    found = jnp.zeros((layers * rows, 3 * block), jnp.float32)
    for index in range(27):
        dx, dy, dz = index // 9 - 1, (index // 3) % 3 - 1, index % 3 - 1
        seen = jnp.concatenate(
            [
                open_ref[(dx + 1) * 4 + layer + 1 + dz, 8 + dy : 40 + dy, :]
                for layer in range(layers)
            ],
            axis=0,
        )
        found = found + jnp.dot(
            seen[:, :32].astype(jnp.bfloat16),
            select_ref[index],
            preferred_element_type=jnp.float32,
        )
    wide_lane = lax.broadcasted_iota(jnp.int32, (layers * rows, block), 1)
    start = found[:, :block]
    length = found[:, block : 2 * block] * (
        found[:, 2 * block :] + jnp.where(wide_lane == 0, 1.0, 0.0)
    )
    before = jnp.where(
        lax.broadcasted_iota(jnp.int32, (block, block), 0)
        < lax.broadcasted_iota(jnp.int32, (block, block), 1),
        1.0,
        0.0,
    ).astype(jnp.bfloat16)
    ahead = jnp.dot(length.astype(jnp.bfloat16), before, preferred_element_type=jnp.float32)
    first_int = start.astype(jnp.int32)
    ahead_int = ahead.astype(jnp.int32)
    moves = (ahead_int - first_int) & (block - 1)
    plan_ref[0 : layers * rows, :] = jnp.where(wide_lane == LIVE_LANE, first_int, moves)
    plan_ref[layers * rows :, :] = ahead_int
    plans = pltpu.make_async_copy(plan_ref, steps_ref, steps_sem)
    plans.start()

    tile = (8, block)
    lane = lax.broadcasted_iota(jnp.int32, tile, 1)
    sub = lax.broadcasted_iota(jnp.int32, tile, 0)

    def fill(group, carry):
        place, first = group // 4, pl.multiple_of((group % 4) * 8, 8)
        parts = [ghost_ref[place, pl.ds(c * rows + first, 8), :] for c in range(4)]
        values = parts[:3] + looked_up(parts[3], (sigma_ref, epsilon_ref, charge_ref))
        for c, value in enumerate(values):
            far_ref[group // 16, pl.ds((group % 16) * 64 + c, 8, stride=8), :] = value
        return carry

    lax.fori_loop(0, places * rows // 8, fill, 0, unroll=2)
    for index in range(27):
        step = (index // 9 - 1, (index // 3) % 3 - 1, index % 3 - 1)
        shift_ref[index * 8 : index * 8 + 8, :] = jnp.where(
            sub == 0,
            float(step[0]),
            jnp.where(sub == 1, float(step[1]), jnp.where(sub == 2, float(step[2]), 0.0)),
        )
    turned_ref[...] = jnp.zeros(turned_ref.shape, jnp.float32)
    piece = lax.broadcasted_iota(jnp.int32, (32, 6 * block), 0)
    column = lax.broadcasted_iota(jnp.int32, (32, 6 * block), 1)
    pick_ref[...] = jnp.where(
        ((piece & 7) == (column >> 7)) & (piece < 24), 1.0, 0.0
    ).astype(jnp.bfloat16)

    plans.wait()

    def lift(cell):
        whole = near_ref[pl.ds(pl.multiple_of(cell * 8, 8), 8), :]
        high = whole.astype(jnp.bfloat16).astype(jnp.float32)
        rest = whole - high
        middle = rest.astype(jnp.bfloat16).astype(jnp.float32)
        parts = jnp.concatenate([high, middle, rest - middle, jnp.zeros(tile, jnp.float32)], axis=0)
        up_ref[...] = jnp.transpose(parts).astype(jnp.bfloat16)

    def collect(cell):
        for b in range(block // 8):
            part = slice(8 * b, 8 * b + 8)
            for c in range(3):
                force = jnp.sum(sum_ref[c, part, :], axis=1, keepdims=True)
                turned_ref[c, part, :] = jnp.where(lane == cell, force, turned_ref[c, part, :])

    def visit(cell, carry):
        layer = cell // rows
        row = cell % rows
        live = steps_ref[cell, LIVE_LANE]
        wide_ref[...] = jnp.dot(up_ref[...], pick_ref[...], preferred_element_type=jnp.float32)
        collect(cell - 1)
        lines = {}
        for dy in (-1, 0, 1):
            line = 8 * (layer * rows + ((row + dy) & (rows - 1)))
            for dz in (-1, 0, 1):
                lines[dy, dz] = pl.multiple_of(line + 8 * rows * (1 + dz), 8)
        for j, ((dx, dy, dz), _, k, _) in enumerate(SEGMENTS):
            filled = steps_ref[layers * rows + cell, j]
            value = far_ref[dx + 1, pl.ds(lines[dy, dz], 8), :]
            if k is not None:
                index = (dx + 1) * 9 + (dy + 1) * 3 + dz + 1
                value = value + shift_ref[index * 8 : index * 8 + 8, :]
            rolled = pltpu.roll(value, steps_ref[cell, j], axis=1)
            place = pl.multiple_of((filled >> 7) << 3, 8)
            list_ref[pl.ds(place + 8, 8), :] = rolled
            pltpu.store(
                list_ref.at[pl.ds(place, 8), :], rolled, mask=lane >= (filled & (block - 1))
            )
        filled = steps_ref[layers * rows + cell, len(SEGMENTS)]
        pltpu.store(
            list_ref.at[pl.ds(pl.multiple_of((filled >> 7) << 3, 8), 8), :],
            jnp.zeros(tile, jnp.float32),
            mask=lane >= (filled & (block - 1)),
        )
        pieces = (filled + block - 1) >> 7
        lift((cell + 1) & (layers * rows - 1))

        def against(blocks):
            def one(piece, first):
                far = [
                    jnp.broadcast_to(list_ref[pl.ds(piece * 8 + c, 1), :], tile) for c in range(6)
                ]
                for b in range(blocks):
                    part = slice(8 * b, 8 * b + 8)
                    near = [wide_ref[part, c * block : (c + 1) * block] for c in range(6)]
                    for c, value in enumerate(pair_force(near, far)):
                        sum_ref[c, part, :] = value if first else sum_ref[c, part, :] + value

            def more(piece, carry):
                one(piece, False)
                return carry

            one(0, True)
            lax.fori_loop(1, pieces, more, 0)

        def choose(options):
            if len(options) == 1:
                against(options[0])
                return
            half = len(options) // 2
            fits = live <= 8 * options[half - 1]
            pl.when(fits)(lambda: choose(options[:half]))
            pl.when(jnp.logical_not(fits))(lambda: choose(options[half:]))

        choose(ROW_BLOCKS)
        return carry

    lift(0)
    lax.fori_loop(0, layers * rows, visit, 0)
    collect(layers * rows - 1)
    present = wide_lane < jnp.broadcast_to(first_int[:, LIVE_LANE : LIVE_LANE + 1], start.shape)
    for c in range(3):
        out_ref[c] = jnp.where(present, jnp.transpose(turned_ref[c])[: layers * rows], 0.0)


def sort_cells(tables, positions, types, counts, flags, sizes=None):
    cells, block = types.shape
    smem = pl.BlockSpec(memory_space=pltpu.SMEM)
    vmem = pl.BlockSpec(memory_space=pltpu.VMEM)
    return pl.pallas_call(
        functools.partial(sort_kernel, sizes=sizes),
        out_shape=(
            jax.ShapeDtypeStruct((12, LAYER_ROWS, block), jnp.float32),
            jax.ShapeDtypeStruct((8 * cells, block), jnp.float32),
        ),
        in_specs=[smem, smem, smem, vmem, vmem, vmem, vmem],
        out_specs=(vmem, vmem),
        scratch_shapes=[
            pltpu.VMEM((16 * cells, block), jnp.float32),
            pltpu.VMEM((cells, block), jnp.float32),
            pltpu.VMEM((cells, block), jnp.float32),
            pltpu.SemaphoreType.DMA((len(ROUTE),)),
            pltpu.SemaphoreType.DMA((len(ROUTE),)),
        ],
        compiler_params=pltpu.CompilerParams(collective_id=0, has_side_effects=True)
        if sizes
        else None,
        name="sort_and_share",
    )(*tables, positions, types, counts, flags)


def pair_forces(tables, ghost, near):
    total_cells, block = ghost.shape[0] * ROWS, ghost.shape[2]
    cells = near.shape[0] // 8
    smem = pl.BlockSpec(memory_space=pltpu.SMEM)
    vmem = pl.BlockSpec(memory_space=pltpu.VMEM)
    return pl.pallas_call(
        pair_kernel,
        out_shape=jax.ShapeDtypeStruct((3, cells, block), jnp.float32),
        in_specs=[smem, smem, smem, vmem, vmem, vmem],
        out_specs=vmem,
        scratch_shapes=[
            pltpu.VMEM((3, 8 * total_cells // 3, block), jnp.float32),
            pltpu.VMEM((27 * 8, block), jnp.float32),
            pltpu.VMEM((29 * 8, block), jnp.float32),
            pltpu.VMEM((block, 6 * block), jnp.float32),
            pltpu.VMEM((32, 6 * block), jnp.bfloat16),
            pltpu.VMEM((block, 32), jnp.bfloat16),
            pltpu.VMEM((3, block, block), jnp.float32),
            pltpu.VMEM((3, block, block), jnp.float32),
            pltpu.VMEM((ghost.shape[0], 48, block), jnp.float32),
            pltpu.VMEM((2 * cells, block), jnp.int32),
            pltpu.SMEM((2 * cells, block), jnp.int32),
            pltpu.SemaphoreType.DMA,
        ],
        name="pair_forces",
    )(*tables, selection(), ghost, near)


def local(positions, atom_types, atom_counts, pair_flags, sigma_table, epsilon_table, charge_table):
    layers, rows, block = positions.shape[2:]
    cells = layers * rows
    tables = (sigma_table, epsilon_table, charge_table)
    ghost, near = sort_cells(
        tables,
        positions.reshape(3, cells, block),
        atom_types.reshape(cells, block),
        atom_counts.reshape(layers, rows),
        pair_flags.reshape(13, layers, rows),
        (lax.axis_size("xy"), lax.axis_size("gz")),
    )
    forces = pair_forces(tables, ghost, near)
    return forces.reshape(3, 1, layers, rows, block)


def solution(mesh):
    return jax.shard_map(
        local,
        mesh=mesh,
        in_specs=(
            P(None, "xy", "gz", None, None),
            P("xy", "gz", None, None),
            P("xy", "gz", None),
            P(None, "xy", "gz", None),
            P(),
            P(),
            P(),
        ),
        out_specs=P(None, "xy", "gz", None, None),
        check_vma=False,
    )
```

```python
import functools

import jax
import jax.numpy as jnp
import numpy as np
from jax import lax
from jax.experimental import pallas as pl
from jax.experimental.pallas import tpu as pltpu
from jax.sharding import PartitionSpec as P

SOFTENING = 0.0125
HALF_SHELL = (
    (0, 0, 1),
    (0, 1, -1),
    (0, 1, 0),
    (0, 1, 1),
    (1, -1, -1),
    (1, -1, 0),
    (1, -1, 1),
    (1, 0, -1),
    (1, 0, 0),
    (1, 0, 1),
    (1, 1, -1),
    (1, 1, 0),
    (1, 1, 1),
)
OCTANTS = (
    (0, 0, 0),
    (0, 0, 1),
    (0, 1, 1),
    (0, 1, 0),
    (1, 1, 0),
    (1, 1, 1),
    (1, 0, 1),
    (1, 0, 0),
)
FLAG_LANE = 16
COUNT_LANE = FLAG_LANE + 13
ROW_BLOCKS = (6, 8, 10, 12, 14, 16)


def octant_runs(offset):
    wanted = [
        all(o == 0 or (o < 0) == bool(bit) for o, bit in zip(offset, octant)) for octant in OCTANTS
    ]
    runs, start = [], None
    for place, keep in enumerate(wanted + [False]):
        if keep and start is None:
            start = place
        if not keep and start is not None:
            runs.append((start, place))
            start = None
    return runs


SEGMENTS = [((0, 0, 0), (0, 8), None, False)]
for _k, _offset in enumerate(HALF_SHELL):
    for _sign in (1, -1):
        _reach = tuple(_sign * o for o in _offset)
        for _run in octant_runs(_reach):
            SEGMENTS.append((_reach, _run, _k, _sign < 0))


LIVE_LANE = 40


def selection():
    table = np.zeros((27, 32, 384), np.float32)
    for j, ((dx, dy, dz), (first, last), k, backward) in enumerate(SEGMENTS):
        offset = (dx + 1) * 9 + (dy + 1) * 3 + dz + 1
        table[offset, first, j] += 1.0
        table[offset, last, 128 + j] += 1.0
        table[offset, first, 128 + j] -= 1.0
        if k is not None:
            table[offset if backward else 13, FLAG_LANE + k, 256 + j] += 1.0
    table[13, 8, LIVE_LANE] += 1.0
    return jnp.asarray(table, jnp.bfloat16)


def looked_up(types, tables):
    values = [jnp.zeros(types.shape, jnp.float32) for _ in tables]
    for t in range(tables[0].shape[0]):
        here = types == t
        values = [jnp.where(here, table[t], value) for table, value in zip(tables, values)]
    sigma, epsilon, charge = values
    return [sigma, jnp.sqrt(32.0 * epsilon), 2.0 * charge]


ROWS = 32
LAYER_ROWS = 4 * ROWS + 8
ROUTE = (
    (0, (0, -1), 5, 7),
    (0, (-1, 0), 5, 9),
    (0, (1, 0), 5, 1),
    (1, (0, 1), 6, 4),
    (1, (-1, 0), 6, 10),
    (1, (1, 0), 6, 2),
    (2, (-1, 0), 7, 11),
    (2, (1, 0), 7, 3),
    (3, (-1, 0), 4, 8),
    (3, (1, 0), 4, 0),
)


def sort_kernel(
    sigma_ref,
    epsilon_ref,
    charge_ref,
    pos_ref,
    type_ref,
    count_ref,
    flag_ref,
    ghost_ref,
    near_ref,
    piece_ref,
    rank_ref,
    meta_ref,
    send_sem,
    recv_sem,
    *,
    sizes,
):
    cells, block = type_ref.shape
    rows = ROWS
    copies = []
    if sizes is not None:
        mine = [lax.axis_index("xy"), lax.axis_index("gz")]

        def at(steps):
            return tuple(lax.rem(m + d + n, n) for m, d, n in zip(mine, steps, sizes))

        barrier = pltpu.get_barrier_semaphore()
        for steps in ((0, -1), (0, 1), (-1, 0), (1, 0)):
            pl.semaphore_signal(
                barrier, inc=1, device_id=at(steps), device_id_type=pl.DeviceIdType.MESH
            )
        for index, (_, steps, source, target) in enumerate(ROUTE):
            copies.append(
                pltpu.make_async_remote_copy(
                    src_ref=ghost_ref.at[source],
                    dst_ref=ghost_ref.at[target],
                    send_sem=send_sem.at[index],
                    recv_sem=recv_sem.at[index],
                    device_id=at(steps),
                    device_id_type=pl.DeviceIdType.MESH,
                )
            )

    def send(stage):
        for copy, message in zip(copies, ROUTE):
            if message[0] == stage:
                copy.start()

    lane = lax.broadcasted_iota(jnp.int32, (cells, block), 1)
    spread_row = lax.broadcasted_iota(jnp.int32, (16, block), 0)
    spread_lane = lax.broadcasted_iota(jnp.int32, (16, block), 1)
    spread = jnp.where(spread_row + FLAG_LANE == spread_lane, 1.0, 0.0).astype(jnp.bfloat16)
    aux = []
    for layer in range(2):
        small = jnp.concatenate(
            [
                flag_ref[:, layer, :].astype(jnp.float32),
                count_ref[layer : layer + 1, :].astype(jnp.float32),
                jnp.zeros((2, rows), jnp.float32),
            ],
            axis=0,
        )
        aux.append(
            lax.dot_general(
                small.astype(jnp.bfloat16),
                spread,
                (((0,), (0,)), ((), ())),
                preferred_element_type=jnp.float32,
            )
        )
    aux = jnp.concatenate(aux, axis=0)
    count = jnp.broadcast_to(aux[:, COUNT_LANE : COUNT_LANE + 1], (cells, block))
    live = lane.astype(jnp.float32) < count
    types = type_ref[...]
    positions = [pos_ref[c] for c in range(3)]
    upper = [jnp.where(p >= 0.5, 1, 0) for p in positions]
    mid = upper[0] ^ upper[1]
    code = 4 * upper[0] + 2 * mid + (mid ^ upper[2])
    code = jnp.where(live, code, 8)
    row_id = lax.broadcasted_iota(jnp.int32, (block, 2 * block), 0)
    lane_id = lax.broadcasted_iota(jnp.int32, (block, 2 * block), 1)
    counting = jnp.where((row_id <= lane_id) | (lane_id >= block), 1.0, 0.0).astype(jnp.bfloat16)
    rank = jnp.zeros((cells, block), jnp.float32)
    offset = jnp.zeros((cells, block), jnp.float32)
    meta = aux
    for b in range(9):
        member = code == b
        found = jnp.dot(
            jnp.where(member, 1.0, 0.0).astype(jnp.bfloat16),
            counting,
            preferred_element_type=jnp.float32,
        )
        rank = jnp.where(member, found[:, :block] - 1.0 + offset, rank)
        meta = jnp.where(lane == b, offset, meta)
        offset = offset + found[:, block:]
    rank_ref[...] = rank
    meta_ref[...] = jnp.where(lane < 32, meta, 0.0)
    for layer in range(2):
        packed = meta_ref[pl.ds(layer * rows, 8, stride=4), :]
        for part in range(1, 4):
            packed = packed + pltpu.roll(
                meta_ref[pl.ds(layer * rows + part, 8, stride=4), :], 32 * part, axis=1
            )
        ghost_ref[5 + layer, 4 * rows : LAYER_ROWS, :] = packed
    zero = jnp.zeros((cells, block), jnp.float32)
    high = [p.astype(jnp.bfloat16).astype(jnp.float32) for p in positions]
    rest = [p - h for p, h in zip(positions, high)]
    middle = [r.astype(jnp.bfloat16).astype(jnp.float32) for r in rest]
    low = [r - m for r, m in zip(rest, middle)]
    pieces = (
        high + [types.astype(jnp.float32)] + middle + [zero] + low + [zero, zero, zero, zero, zero]
    )
    for group in range(cells // 8):
        part = slice(group * 8, group * 8 + 8)
        for c in range(16):
            piece_ref[pl.ds(group * 128 + c, 8, stride=16), :] = pieces[c][part]
    slot = lax.broadcasted_iota(jnp.int32, (block, block), 0).astype(jnp.float32)

    def sort_layer(layer):
        def one(row, carry):
            cell = layer * rows + row
            ranks = jnp.broadcast_to(rank_ref[pl.ds(cell, 1), :], (block, block))
            chosen = jnp.where(ranks == slot, 1.0, 0.0).astype(jnp.bfloat16)
            data = piece_ref[pl.ds(pl.multiple_of(cell * 16, 16), 16), :].astype(jnp.bfloat16)
            moved = lax.dot_general(
                data, chosen, (((1,), (1,)), ((), ())), preferred_element_type=jnp.float32
            )
            whole = (moved[0:4] + moved[4:8]) + moved[8:12]
            for c in range(4):
                ghost_ref[5 + layer, pl.ds(c * rows + row, 1), :] = whole[c : c + 1]
            return carry

        lax.fori_loop(0, rows, one, 0, unroll=16)

    sort_layer(0)
    if copies:
        pl.semaphore_wait(barrier, 4)
    send(0)
    sort_layer(1)
    send(1)
    present = jnp.where(live, 1.0, 0.0)
    kinds = looked_up(types, (sigma_ref, epsilon_ref, charge_ref))
    near = [2.0 * p for p in positions] + [kinds[0], kinds[1] * present, kinds[2] * present, zero, zero]
    for group in range(cells // 8):
        part = slice(group * 8, group * 8 + 8)
        for c in range(8):
            near_ref[pl.ds(group * 64 + c, 8, stride=8), :] = near[c][part]
    if copies:
        copies[0].wait()
        send(2)
        copies[3].wait()
        send(3)
        for index in (1, 2, 4, 5, 6, 7, 8, 9):
            copies[index].wait()


def pair_force(near, far):
    delta = [near[c] - far[c] for c in range(3)]
    dist_sq = delta[0] * delta[0] + delta[1] * delta[1] + delta[2] * delta[2]
    sigma = near[3] + far[3]
    sigma_sq = sigma * sigma
    switch = jnp.maximum(1.0 - dist_sq, 0.0)
    inverse = 1.0 / (dist_sq + sigma_sq)
    quotient = sigma_sq * inverse
    power = quotient * quotient * quotient
    less = power - 1.0
    softened = dist_sq + 4.0 * SOFTENING
    inverse_radius = lax.rsqrt(softened)
    reach = (softened * inverse_radius) * -2.0
    lennard = ((near[4] * far[4]) * power) * (less + ((1.5 * switch) * inverse) * (less + power))
    coulomb = ((near[5] * far[5]) * (jnp.exp(reach) * inverse_radius)) * (
        4.0 + (switch * (1.0 - reach)) * (inverse_radius * inverse_radius)
    )
    scalar = (lennard + coulomb) * switch
    return [scalar * d for d in delta]


def pair_kernel(
    sigma_ref,
    epsilon_ref,
    charge_ref,
    select_ref,
    ghost_ref,
    near_ref,
    out_ref,
    far_ref,
    shift_ref,
    list_ref,
    wide_ref,
    pick_ref,
    up_ref,
    sum_ref,
    turned_ref,
    open_ref,
    plan_ref,
    steps_ref,
    steps_sem,
):
    layers, rows = 2, ROWS
    block = 128
    places = ghost_ref.shape[0]
    for place in range(places):
        packed = ghost_ref[place, 4 * rows : LAYER_ROWS, :]
        for part in range(4):
            turned = pltpu.roll(packed, (block - 32 * part) % block, axis=1) if part else packed
            open_ref[place, pl.ds(8 + part, 8, stride=4), :] = turned
        open_ref[place, 7:8, :] = open_ref[place, 39:40, :]
        open_ref[place, 40:41, :] = open_ref[place, 8:9, :]
    found = jnp.zeros((layers * rows, 3 * block), jnp.float32)
    for index in range(27):
        dx, dy, dz = index // 9 - 1, (index // 3) % 3 - 1, index % 3 - 1
        seen = jnp.concatenate(
            [
                open_ref[(dx + 1) * 4 + layer + 1 + dz, 8 + dy : 40 + dy, :]
                for layer in range(layers)
            ],
            axis=0,
        )
        found = found + jnp.dot(
            seen[:, :32].astype(jnp.bfloat16),
            select_ref[index],
            preferred_element_type=jnp.float32,
        )
    wide_lane = lax.broadcasted_iota(jnp.int32, (layers * rows, block), 1)
    start = found[:, :block]
    length = found[:, block : 2 * block] * (
        found[:, 2 * block :] + jnp.where(wide_lane == 0, 1.0, 0.0)
    )
    before = jnp.where(
        lax.broadcasted_iota(jnp.int32, (block, block), 0)
        < lax.broadcasted_iota(jnp.int32, (block, block), 1),
        1.0,
        0.0,
    ).astype(jnp.bfloat16)
    ahead = jnp.dot(length.astype(jnp.bfloat16), before, preferred_element_type=jnp.float32)
    first_int = start.astype(jnp.int32)
    ahead_int = ahead.astype(jnp.int32)
    moves = (ahead_int - first_int) & (block - 1)
    plan_ref[0 : layers * rows, :] = jnp.where(wide_lane == LIVE_LANE, first_int, moves)
    plan_ref[layers * rows :, :] = ahead_int
    plans = pltpu.make_async_copy(plan_ref, steps_ref, steps_sem)
    plans.start()

    tile = (8, block)
    lane = lax.broadcasted_iota(jnp.int32, tile, 1)
    sub = lax.broadcasted_iota(jnp.int32, tile, 0)

    def fill(group, carry):
        place, first = group // 4, pl.multiple_of((group % 4) * 8, 8)
        parts = [ghost_ref[place, pl.ds(c * rows + first, 8), :] for c in range(4)]
        values = [2.0 * part for part in parts[:3]] + looked_up(parts[3], (sigma_ref, epsilon_ref, charge_ref))
        for c, value in enumerate(values):
            far_ref[group // 16, pl.ds((group % 16) * 64 + c, 8, stride=8), :] = value
        return carry

    lax.fori_loop(0, places * rows // 8, fill, 0, unroll=4)
    for index in range(27):
        step = (index // 9 - 1, (index // 3) % 3 - 1, index % 3 - 1)
        shift_ref[index * 8 : index * 8 + 8, :] = jnp.where(
            sub == 0,
            2.0 * step[0],
            jnp.where(sub == 1, 2.0 * step[1], jnp.where(sub == 2, 2.0 * step[2], 0.0)),
        )
    turned_ref[...] = jnp.zeros(turned_ref.shape, jnp.float32)
    piece = lax.broadcasted_iota(jnp.int32, (32, 6 * block), 0)
    column = lax.broadcasted_iota(jnp.int32, (32, 6 * block), 1)
    pick_ref[...] = jnp.where(
        ((piece & 7) == (column >> 7)) & (piece < 24), 1.0, 0.0
    ).astype(jnp.bfloat16)

    plans.wait()

    def lift(cell):
        whole = near_ref[pl.ds(pl.multiple_of(cell * 8, 8), 8), :]
        high = whole.astype(jnp.bfloat16).astype(jnp.float32)
        rest = whole - high
        middle = rest.astype(jnp.bfloat16).astype(jnp.float32)
        parts = jnp.concatenate([high, middle, rest - middle, jnp.zeros(tile, jnp.float32)], axis=0)
        up_ref[...] = jnp.transpose(parts).astype(jnp.bfloat16)

    def collect(cell):
        for b in range(block // 8):
            part = slice(8 * b, 8 * b + 8)
            for c in range(3):
                force = jnp.sum(sum_ref[c, part, :], axis=1, keepdims=True)
                turned_ref[c, part, :] = jnp.where(lane == cell, force, turned_ref[c, part, :])

    def visit(cell, carry):
        layer = cell // rows
        row = cell % rows
        live = steps_ref[cell, LIVE_LANE]
        wide_ref[...] = jnp.dot(up_ref[...], pick_ref[...], preferred_element_type=jnp.float32)
        collect(cell - 1)
        lines = {}
        for dy in (-1, 0, 1):
            line = 8 * (layer * rows + ((row + dy) & (rows - 1)))
            for dz in (-1, 0, 1):
                lines[dy, dz] = pl.multiple_of(line + 8 * rows * (1 + dz), 8)
        for j, ((dx, dy, dz), _, k, _) in enumerate(SEGMENTS):
            filled = steps_ref[layers * rows + cell, j]
            value = far_ref[dx + 1, pl.ds(lines[dy, dz], 8), :]
            if k is not None:
                index = (dx + 1) * 9 + (dy + 1) * 3 + dz + 1
                value = value + shift_ref[index * 8 : index * 8 + 8, :]
            rolled = pltpu.roll(value, steps_ref[cell, j], axis=1)
            place = pl.multiple_of((filled >> 7) << 3, 8)
            list_ref[pl.ds(place + 8, 8), :] = rolled
            pltpu.store(
                list_ref.at[pl.ds(place, 8), :], rolled, mask=lane >= (filled & (block - 1))
            )
        filled = steps_ref[layers * rows + cell, len(SEGMENTS)]
        pltpu.store(
            list_ref.at[pl.ds(pl.multiple_of((filled >> 7) << 3, 8), 8), :],
            jnp.zeros(tile, jnp.float32),
            mask=lane >= (filled & (block - 1)),
        )
        pieces = (filled + block - 1) >> 7
        lift((cell + 1) & (layers * rows - 1))

        def against(blocks):
            def one(piece, first):
                far = [
                    jnp.broadcast_to(list_ref[pl.ds(piece * 8 + c, 1), :], tile) for c in range(6)
                ]
                for b in range(blocks):
                    part = slice(8 * b, 8 * b + 8)
                    near = [wide_ref[part, c * block : (c + 1) * block] for c in range(6)]
                    for c, value in enumerate(pair_force(near, far)):
                        sum_ref[c, part, :] = value if first else sum_ref[c, part, :] + value

            def more(piece, carry):
                one(piece, False)
                return carry

            one(0, True)
            lax.fori_loop(1, pieces, more, 0)

        def choose(options):
            if len(options) == 1:
                against(options[0])
                return
            half = len(options) // 2
            fits = live <= 8 * options[half - 1]
            pl.when(fits)(lambda: choose(options[:half]))
            pl.when(jnp.logical_not(fits))(lambda: choose(options[half:]))

        choose(ROW_BLOCKS)
        return carry

    lift(0)
    lax.fori_loop(0, layers * rows, visit, 0)
    collect(layers * rows - 1)
    present = wide_lane < jnp.broadcast_to(first_int[:, LIVE_LANE : LIVE_LANE + 1], start.shape)
    for c in range(3):
        out_ref[c] = jnp.where(present, jnp.transpose(turned_ref[c])[: layers * rows], 0.0)


def sort_cells(tables, positions, types, counts, flags, sizes=None):
    cells, block = types.shape
    smem = pl.BlockSpec(memory_space=pltpu.SMEM)
    vmem = pl.BlockSpec(memory_space=pltpu.VMEM)
    return pl.pallas_call(
        functools.partial(sort_kernel, sizes=sizes),
        out_shape=(
            jax.ShapeDtypeStruct((12, LAYER_ROWS, block), jnp.float32),
            jax.ShapeDtypeStruct((8 * cells, block), jnp.float32),
        ),
        in_specs=[smem, smem, smem, vmem, vmem, vmem, vmem],
        out_specs=(vmem, vmem),
        scratch_shapes=[
            pltpu.VMEM((16 * cells, block), jnp.float32),
            pltpu.VMEM((cells, block), jnp.float32),
            pltpu.VMEM((cells, block), jnp.float32),
            pltpu.SemaphoreType.DMA((len(ROUTE),)),
            pltpu.SemaphoreType.DMA((len(ROUTE),)),
        ],
        compiler_params=pltpu.CompilerParams(collective_id=0, has_side_effects=True)
        if sizes
        else None,
        name="sort_and_share",
    )(*tables, positions, types, counts, flags)


def pair_forces(tables, ghost, near):
    total_cells, block = ghost.shape[0] * ROWS, ghost.shape[2]
    cells = near.shape[0] // 8
    smem = pl.BlockSpec(memory_space=pltpu.SMEM)
    vmem = pl.BlockSpec(memory_space=pltpu.VMEM)
    return pl.pallas_call(
        pair_kernel,
        out_shape=jax.ShapeDtypeStruct((3, cells, block), jnp.float32),
        in_specs=[smem, smem, smem, vmem, vmem, vmem],
        out_specs=vmem,
        scratch_shapes=[
            pltpu.VMEM((3, 8 * total_cells // 3, block), jnp.float32),
            pltpu.VMEM((27 * 8, block), jnp.float32),
            pltpu.VMEM((29 * 8, block), jnp.float32),
            pltpu.VMEM((block, 6 * block), jnp.float32),
            pltpu.VMEM((32, 6 * block), jnp.bfloat16),
            pltpu.VMEM((block, 32), jnp.bfloat16),
            pltpu.VMEM((3, block, block), jnp.float32),
            pltpu.VMEM((3, block, block), jnp.float32),
            pltpu.VMEM((ghost.shape[0], 48, block), jnp.float32),
            pltpu.VMEM((2 * cells, block), jnp.int32),
            pltpu.SMEM((2 * cells, block), jnp.int32),
            pltpu.SemaphoreType.DMA,
        ],
        name="pair_forces",
    )(*tables, selection(), ghost, near)


def local(positions, atom_types, atom_counts, pair_flags, sigma_table, epsilon_table, charge_table):
    layers, rows, block = positions.shape[2:]
    cells = layers * rows
    tables = (sigma_table, epsilon_table, charge_table)
    ghost, near = sort_cells(
        tables,
        positions.reshape(3, cells, block),
        atom_types.reshape(cells, block),
        atom_counts.reshape(layers, rows),
        pair_flags.reshape(13, layers, rows),
        (lax.axis_size("xy"), lax.axis_size("gz")),
    )
    forces = pair_forces(tables, ghost, near)
    return forces.reshape(3, 1, layers, rows, block)


def solution(mesh):
    return jax.shard_map(
        local,
        mesh=mesh,
        in_specs=(
            P(None, "xy", "gz", None, None),
            P("xy", "gz", None, None),
            P("xy", "gz", None),
            P(None, "xy", "gz", None),
            P(),
            P(),
            P(),
        ),
        out_specs=P(None, "xy", "gz", None, None),
        check_vma=False,
    )
```
